1024 devices in a mesh: dp: 32 (over y, z_hi, core), cuts: 32 (over z_lo, x).
Axes of the slice: x: 4, y: 8, z: 16 (z_hi: 2, z_lo: 8; z = z_hi * 8 + z_lo), core: 2. Of those that a mesh axis runs over, the one named last changes fastest.
Arguments:
- hidden: bfloat16 [32, 256, 8192], P('dp', None, 'cuts'), may hold values from -6 to 6
- down_weight: bfloat16 [32, 8192, 3072], P('dp', 'cuts'), may hold values from -0.0625 to 0.0625
- expert_ids: int32 [4096, 2], P('dp'), may hold values from 0 to 63, all different within a row; in each aligned block of 128 rows (0 to 127, 128 to 255, ...) at most 8 rows name the same one
- combine: float32 [4096, 2], P('dp'), may hold values from 0.1 to 1
- out_grad: bfloat16 [4096, 3072], P('dp', 'cuts'), may hold values from -6 to 6
Outputs:
- mixed: bfloat16 [4096, 3072], P('dp', 'cuts')
- hidden_grad: bfloat16 [32, 256, 8192], P('dp', None, 'cuts')
- weight_grad: bfloat16 [32, 8192, 3072], P('dp', 'cuts')
The draws below stay inside these ranges and needn't reach their ends.
Inputs may be any that keep to these rules, and one draw needn't show every extreme that they name: `expert_ids`: the two ids of a row differ. Among the 256 pairs of one index of dp, no expert is named more than 8 times, a bound that some block reaches.
All inputs are finite; a program needn't handle non-finite values.
Results may differ from the reference program's by a relative error of at most 0.0049.
Values may be sent and summed in bfloat16 or wider, within the bound.
A program may use at most 32 MiB of HBM per device.

```python
import math
import jax
import jax.numpy as jnp
import numpy as np
from jax import lax

D = 3072
FF = 8192
T_DP = 128
TOKENS = 4096
EXPERTS = 64
WINDOW = 32
CAP = 8
SLOTS = 256
N_DP = 32


def block_scale(rng, shape, split, low, top_value):
    level, own = 1.0, jax.random.fold_in(rng, 6)
    for position, parts in split:
        draws = jnp.exp(jax.random.uniform(jax.random.fold_in(own, position), (parts,), jnp.float32, low / len(split), top_value / len(split)))
        level = level * jnp.repeat(draws, shape[position] // parts).reshape([-1 if axis == position else 1 for axis in range(len(shape))])
    return level


def assign_block(stream_key, own, number, rows, amount, top, limit, slope):
    sequence = jax.random.permutation(stream_key, amount)
    crowded, common = load_shares(amount, rows * top, limit, slope, True), load_shares(amount, rows * top, limit, slope, False)
    places = jnp.arange(amount)

    def named(sizes, offset_by):
        used = int((sizes > 0).sum())
        fixed = max(1, used // 4)
        moved = fixed + (places - fixed + offset_by * (used - fixed)) % max(1, amount - fixed)
        return jnp.zeros((amount,), jnp.int32).at[sequence[jnp.where(places < fixed, places, moved)]].set(jnp.asarray(sizes, jnp.int32))

    sizes = jnp.where(number % 4 == 0, named(crowded, number // 4), named(common, number - number // 4 - 1))
    mixed = jax.random.permutation(jax.random.fold_in(own, 3), amount)
    source_of, receiver = mixed[0:amount // 2 * 2:2], mixed[1:amount // 2 * 2:2]
    margin = jnp.minimum(sizes[source_of] - 1, limit - sizes[receiver]) // 2
    margin = jnp.where((source_of == sequence[0]) | (receiver == sequence[0]) | (sizes[receiver] == 0), 0, jnp.maximum(margin, 0))
    moved = jax.random.randint(jax.random.fold_in(own, 4), (amount // 2,), 0, 1 << 20) % (margin + 1)
    sizes = sizes.at[source_of].add(-moved).at[receiver].add(moved)
    members = jnp.searchsorted(jnp.cumsum(sizes), jnp.arange(rows * top), side="right").astype(jnp.int32)
    listing = members.reshape(top, rows).T
    listing = listing[jax.random.permutation(jax.random.fold_in(own, 1), rows)]
    offset_by = jax.random.randint(jax.random.fold_in(own, 2), (rows, 1), 0, top)
    return jnp.take_along_axis(listing, (jnp.arange(top)[None, :] + offset_by) % top, axis=1)


def load_shares(count, total, bound, skew, full):
    portions = [(1 << 20) // math.isqrt(standing ** skew) + 1 for standing in range(1, count + 1)]
    largest = bound if full else min(bound, max(-(-total // count), total * portions[0] // sum(portions)))
    least = 1 if total - largest >= count - 1 else 0
    counts, spare = [largest] + [least] * (count - 1), total - largest - least * (count - 1)
    while spare > 0:
        candidates = [i for i in range(1, count) if counts[i] < largest] or [i for i in range(1, count) if counts[i] < bound]
        pool, remaining = sum([portions[i] for i in candidates]), spare
        for i in candidates:
            extra = min(bound - counts[i], max(1, remaining * portions[i] // pool), spare)
            counts[i] = counts[i] + extra
            spare = spare - extra
    return np.array(counts)


def centred(stream_key, shape, deviation, reach, split=(), kind=jnp.bfloat16):
    values = deviation * jax.random.normal(stream_key, shape, jnp.float32)
    if split:
        values = values * block_scale(stream_key, shape, split, -0.22, 0.18)
    return jnp.clip(values, -reach, reach).astype(kind)


def setup_inputs(seed: int = 0) -> dict:
    key_list = jax.random.split(jax.random.key(seed), 6)
    hidden = centred(key_list[0], (WINDOW, SLOTS, FF), 1.0, 6.0, ((0, 32), (2, 32)))
    down_weight = centred(key_list[1], (WINDOW, FF, D), FF ** -0.5, 0.0625, ((0, 32), (1, 32)))
    expert_ids_keys = jax.random.split(jax.random.fold_in(key_list[2], 1), TOKENS // T_DP)
    expert_ids_turns = jax.random.permutation(jax.random.fold_in(key_list[2], 3), TOKENS // T_DP)
    expert_ids = jax.vmap(lambda own, number: assign_block(jax.random.fold_in(key_list[2], 2), own, number, T_DP, EXPERTS, 2, CAP, 2))(expert_ids_keys, expert_ids_turns).reshape((TOKENS, 2))
    combine = jnp.clip(0.1 + 0.9 * jax.random.uniform(key_list[3], (TOKENS, 2), jnp.float32) ** block_scale(key_list[3], (TOKENS, 2), ((0, 32),), -0.2, 0.2), 0.1, 1.0)
    out_grad = centred(key_list[4], (TOKENS, D), 1.0, 6.0, ((0, 32), (1, 32)))
    return dict(hidden=hidden, down_weight=down_weight, expert_ids=expert_ids, combine=combine, out_grad=out_grad)


def reference(hidden, down_weight, expert_ids, combine, out_grad):
    pair_ids = expert_ids.reshape(N_DP, 2 * T_DP).astype(jnp.int32)
    labels = jnp.arange(WINDOW, dtype=jnp.int32)
    onehot = (pair_ids[:, :, None] == labels[None, None, :]).astype(jnp.int32)
    pair_rank = jnp.sum((jnp.cumsum(onehot, axis=1) - 1) * onehot, axis=2)
    block_base = jnp.arange(N_DP, dtype=jnp.int32)[:, None] * CAP
    slot_index = (block_base + pair_rank).reshape(-1).astype(jnp.int32)
    flat_ids = pair_ids.reshape(-1)
    inside = flat_ids < WINDOW
    weights = combine.reshape(-1)
    repeated = jnp.repeat(out_grad, 2, axis=0).astype(jnp.float32)
    pair_grad = (weights[:, None] * repeated).astype(jnp.bfloat16)

    def per_expert(expert_items):
        expert_index, hidden_rows, weight = expert_items
        target = jnp.where(flat_ids == expert_index, slot_index, SLOTS).astype(jnp.int32)
        grad_rows = jnp.zeros((SLOTS, D), jnp.bfloat16).at[target].set(pair_grad, mode="drop")
        hid_grad = jnp.dot(grad_rows, weight.T, preferred_element_type=jnp.float32).astype(jnp.bfloat16)
        down_grad = jnp.dot(hidden_rows.T, grad_rows, preferred_element_type=jnp.float32).astype(jnp.bfloat16)
        out_rows = jnp.dot(hidden_rows, weight, preferred_element_type=jnp.float32).astype(jnp.bfloat16)
        return out_rows, hid_grad, down_grad

    out_rows, hidden_grad, weight_grad = lax.map(per_expert, (labels, hidden, down_weight))
    flat_rows = out_rows.reshape(WINDOW * SLOTS, D)
    pick_index = jnp.where(inside, flat_ids * SLOTS + slot_index, 0).astype(jnp.int32)
    picked = jnp.take(flat_rows, pick_index, axis=0).astype(jnp.float32)
    pair_coef = jnp.where(inside, weights, jnp.zeros_like(weights))
    mixed = jnp.sum((pair_coef[:, None] * picked).reshape(TOKENS, 2, D), axis=1).astype(jnp.bfloat16)
    return (mixed, hidden_grad, weight_grad)
```

```python
import functools

import jax
import jax.numpy as jnp
from jax import lax
from jax.experimental import pallas as pl
from jax.experimental.pallas import tpu as pltpu
from jax.sharding import PartitionSpec as P

MESH = pl.DeviceIdType.MESH
NX = 4
CAP = 8
BF = jnp.bfloat16
F32 = jnp.float32


def split_sum(onehot, rows):
    high = rows.astype(BF)
    low = (rows - high.astype(F32)).astype(BF)
    return jnp.dot(onehot, high, preferred_element_type=F32) + jnp.dot(
        onehot, low, preferred_element_type=F32
    )


def kernel(
    ndp,
    ncuts,
    hid_ref,
    weight_ref,
    term_ref,
    ids_ref,
    comb_ref,
    grad_ref,
    mixed_ref,
    hgrad_ref,
    wgrad_ref,
    out_buf,
    in_buf,
    gath,
    xrecv,
    xsum,
    zrecv,
    back_out,
    back_in,
    a_send,
    a_recv,
    c_send,
    c_recv,
    gz_send,
    gz_recv,
    gx_send,
    gx_recv,
    rx_send,
    rx_recv,
    rz_send,
    rz_recv,
):
    nz = ncuts // NX
    d = lax.axis_index("dp")
    c = lax.axis_index("cuts")
    z = c // NX
    x = lax.rem(c, NX)
    toks, share = grad_ref.shape
    slots = ndp * CAP

    def dp_peer(i):
        return lax.rem(d + i, ndp)

    def z_peer(i):
        return lax.rem(z + i, nz)

    def x_peer(i):
        return lax.rem(x + i, NX)

    barrier = pltpu.get_barrier_semaphore()

    def greet(i, carry):
        pl.semaphore_signal(barrier, inc=1, device_id={"dp": dp_peer(i)}, device_id_type=MESH)
        return carry

    lax.fori_loop(1, ndp, greet, 0)
    for i in range(1, nz):
        pl.semaphore_signal(
            barrier, inc=1, device_id={"cuts": z_peer(i) * NX + x}, device_id_type=MESH
        )
    for i in range(1, NX):
        pl.semaphore_signal(
            barrier, inc=1, device_id={"cuts": z * NX + x_peer(i)}, device_id_type=MESH
        )

    lane = lax.broadcasted_iota(jnp.int32, (toks, 128), 1)
    ids0 = ids_ref[:, 0:1]
    ids1 = ids_ref[:, 1:2]
    named0 = (lane == ids0) & (lane < ndp)
    named1 = (lane == ids1) & (lane < ndp)
    named = jnp.where(named0 | named1, 1.0, 0.0).astype(BF)
    row = lax.broadcasted_iota(jnp.int32, (toks, toks), 0)
    col = lax.broadcasted_iota(jnp.int32, (toks, toks), 1)
    before = jnp.where(col < row, 1.0, 0.0).astype(BF)
    count = jnp.dot(before, named, preferred_element_type=F32)
    rank0 = jnp.sum(jnp.where(named0, count, 0.0), axis=1, keepdims=True).astype(jnp.int32)
    rank1 = jnp.sum(jnp.where(named1, count, 0.0), axis=1, keepdims=True).astype(jnp.int32)
    place = lax.broadcasted_iota(jnp.int32, (toks, slots), 1)
    pick0 = jnp.where(place == ids0 * CAP + rank0, 1.0, 0.0)
    pick1 = jnp.where(place == ids1 * CAP + rank1, 1.0, 0.0)
    comb0 = comb_ref[:, 0:1]
    comb1 = comb_ref[:, 1:2]
    grad = grad_ref[...].astype(F32)
    scaled0 = (grad * comb0).astype(BF)
    scaled1 = (grad * comb1).astype(BF)
    rows = jnp.dot(pick0.T.astype(BF), scaled0, preferred_element_type=F32) + jnp.dot(
        pick1.T.astype(BF), scaled1, preferred_element_type=F32
    )
    out_buf[...] = jnp.zeros_like(out_buf)
    out_buf[:, :, :share] = rows.reshape(ndp, CAP, share)
    back_out[...] = jnp.zeros_like(back_out)

    pl.semaphore_wait(barrier, ndp - 1 + nz - 1 + NX - 1)

    def dp_copy(src, dst, send, recv, i):
        return pltpu.make_async_remote_copy(
            src_ref=src.at[dp_peer(i)],
            dst_ref=dst.at[d],
            send_sem=send.at[i],
            recv_sem=recv.at[d],
            device_id={"dp": dp_peer(i)},
            device_id_type=MESH,
        )

    def dp_arrival(src, dst, send, recv, i):
        return pltpu.make_async_remote_copy(
            src_ref=src.at[d],
            dst_ref=dst.at[dp_peer(i)],
            send_sem=send.at[i],
            recv_sem=recv.at[dp_peer(i)],
            device_id={"dp": dp_peer(i)},
            device_id_type=MESH,
        )

    def dp_start(src, dst, send, recv):
        def body(i, carry):
            dp_copy(src, dst, send, recv, i).start()
            return carry

        lax.fori_loop(1, ndp, body, 0)
        dst[d] = src[d]

    def dp_wait_recv(src, dst, send, recv):
        def body(i, carry):
            dp_arrival(src, dst, send, recv, i).wait_recv()
            return carry

        lax.fori_loop(1, ndp, body, 0)

    def dp_wait_send(src, dst, send, recv):
        def body(i, carry):
            dp_copy(src, dst, send, recv, i).wait_send()
            return carry

        lax.fori_loop(1, ndp, body, 0)

    def rx_copy(i, j):
        zz = z_peer(j)
        return pltpu.make_async_remote_copy(
            src_ref=term_ref.at[zz * NX + x_peer(i)],
            dst_ref=xrecv.at[i, j],
            send_sem=rx_send.at[i, j],
            recv_sem=rx_recv.at[i, j],
            device_id={"cuts": z * NX + x_peer(i)},
            device_id_type=MESH,
        )

    def rz_copy(j):
        return pltpu.make_async_remote_copy(
            src_ref=xsum.at[j],
            dst_ref=zrecv.at[j],
            send_sem=rz_send.at[j],
            recv_sem=rz_recv.at[j],
            device_id={"cuts": z_peer(j) * NX + x},
            device_id_type=MESH,
        )

    def gz_copy(j):
        return pltpu.make_async_remote_copy(
            src_ref=gath.at[c],
            dst_ref=gath.at[c],
            send_sem=gz_send.at[j],
            recv_sem=gz_recv.at[j],
            device_id={"cuts": z_peer(j) * NX + x},
            device_id_type=MESH,
        )

    def gz_arrival(j):
        block = lax.rem(z + nz - j, nz) * NX + x
        return pltpu.make_async_remote_copy(
            src_ref=gath.at[c],
            dst_ref=gath.at[block],
            send_sem=gz_send.at[j],
            recv_sem=gz_recv.at[j],
            device_id={"cuts": z_peer(j) * NX + x},
            device_id_type=MESH,
        )

    def gx_copy(i, j):
        block = lax.rem(z + nz - j, nz) * NX + x
        return pltpu.make_async_remote_copy(
            src_ref=gath.at[block],
            dst_ref=gath.at[block],
            send_sem=gx_send.at[i, j],
            recv_sem=gx_recv.at[i, j],
            device_id={"cuts": z * NX + x_peer(i)},
            device_id_type=MESH,
        )

    def gx_arrival(i, j):
        block = lax.rem(z + nz - j, nz) * NX + lax.rem(x + NX - i, NX)
        return pltpu.make_async_remote_copy(
            src_ref=gath.at[block],
            dst_ref=gath.at[block],
            send_sem=gx_send.at[i, j],
            recv_sem=gx_recv.at[i, j],
            device_id={"cuts": z * NX + x_peer(i)},
            device_id_type=MESH,
        )

    dp_start(out_buf, in_buf, a_send, a_recv)
    z_order = ZORDER(nz)
    for j in z_order + [0]:
        for i in (2, 1, 3):
            rx_copy(i, j).start()

    dp_wait_recv(out_buf, in_buf, a_send, a_recv)
    arrived = in_buf[...].reshape(slots, 128).T
    gath[c] = arrived[:share].astype(BF)
    for j in z_order:
        gz_copy(j).start()
    for i in (2, 1, 3):
        gx_copy(i, 0).start()

    for j in z_order:
        for i in range(1, NX):
            rx_copy(i, j).wait_recv()
        total = term_ref[z_peer(j) * NX + x].astype(F32)
        for i in range(1, NX):
            total = total + xrecv[i, j].astype(F32)
        xsum[j] = total.astype(BF)
        rz_copy(j).start()
    for i in range(1, NX):
        rx_copy(i, 0).wait_recv()
    own = term_ref[c].astype(F32)
    for i in range(1, NX):
        own = own + xrecv[i, 0].astype(F32)

    for j in z_order[::-1]:
        gz_arrival(j).wait_recv()
        for i in (2, 1, 3):
            gx_copy(i, j).start()

    for j in range(1, nz):
        rz_copy(j).wait_recv()
        own = own + zrecv[j].astype(F32)
    back_out[:, :, :share] = own.T.reshape(ndp, CAP, share)
    dp_start(back_out, back_in, c_send, c_recv)

    for j in range(nz):
        for i in range(1, NX):
            gx_arrival(i, j).wait_recv()
    width = ncuts * share
    full = gath[...].reshape(width, slots)
    hgrad_ref[...] = (
        jnp.dot(weight_ref[...], full, preferred_element_type=F32).T.astype(BF)
    )
    hid_t = hid_ref[...].astype(F32).T.astype(BF)
    step = width // 4
    for k in range(4):
        wgrad_ref[:, k * step : (k + 1) * step] = lax.dot_general(
            hid_t,
            full[k * step : (k + 1) * step],
            (((1,), (1,)), ((), ())),
            preferred_element_type=F32,
        ).astype(BF)

    dp_wait_recv(back_out, back_in, c_send, c_recv)
    expert_rows = back_in[...].reshape(slots, 128)
    mixed = comb0 * split_sum(pick0.astype(BF), expert_rows) + comb1 * split_sum(
        pick1.astype(BF), expert_rows
    )
    mixed_ref[...] = mixed[:, :share].astype(BF)

    dp_wait_send(out_buf, in_buf, a_send, a_recv)
    dp_wait_send(back_out, back_in, c_send, c_recv)
    for j in range(nz):
        if j:
            gz_copy(j).wait_send()
            rz_copy(j).wait_send()
        for i in range(1, NX):
            gx_copy(i, j).wait_send()
            rx_copy(i, j).wait_send()


def ZORDER(nz):
    return sorted(range(1, nz), key=lambda j: -min(j, nz - j))


def local(hidden, down_weight, expert_ids, combine, out_grad):
    ndp = lax.axis_size("dp")
    ncuts = lax.axis_size("cuts")
    nz = ncuts // NX
    toks, share = out_grad.shape
    hid = hidden[0]
    weight = down_weight[0]
    slots, ff = hid.shape
    width = weight.shape[1]
    terms = lax.dot_general(
        weight, hid, (((0,), (1,)), ((), ())), preferred_element_type=F32
    ).astype(BF)
    vm = pl.BlockSpec(memory_space=pltpu.VMEM)
    dma = pltpu.SemaphoreType.DMA
    mixed, hgrad, wgrad = pl.pallas_call(
        functools.partial(kernel, ndp, ncuts),
        out_shape=(
            jax.ShapeDtypeStruct((toks, share), BF),
            jax.ShapeDtypeStruct((slots, ff), BF),
            jax.ShapeDtypeStruct((ff, width), BF),
        ),
        in_specs=[vm] * 6,
        out_specs=(vm, vm, vm),
        scratch_shapes=[
            pltpu.VMEM((ndp, CAP, 128), F32),
            pltpu.VMEM((ndp, CAP, 128), F32),
            pltpu.VMEM((ncuts, share, slots), BF),
            pltpu.VMEM((NX, nz, share, slots), BF),
            pltpu.VMEM((nz, share, slots), BF),
            pltpu.VMEM((nz, share, slots), BF),
            pltpu.VMEM((ndp, CAP, 128), F32),
            pltpu.VMEM((ndp, CAP, 128), F32),
            dma((ndp,)),
            dma((ndp,)),
            dma((ndp,)),
            dma((ndp,)),
            dma((nz,)),
            dma((nz,)),
            dma((NX, nz)),
            dma((NX, nz)),
            dma((NX, nz)),
            dma((NX, nz)),
            dma((nz,)),
            dma((nz,)),
        ],
        compiler_params=pltpu.CompilerParams(collective_id=0, has_side_effects=True),
    )(hid, weight, terms.reshape(ncuts, share, slots), expert_ids, combine, out_grad)
    return (mixed, hgrad[None], wgrad[None])


def solution(mesh):
    return jax.shard_map(
        local,
        mesh=mesh,
        in_specs=(
            P("dp", None, "cuts"),
            P("dp", "cuts", None),
            P("dp", None),
            P("dp", None),
            P("dp", "cuts"),
        ),
        out_specs=(P("dp", "cuts"), P("dp", None, "cuts"), P("dp", "cuts", None)),
        check_vma=False,
    )
```

```python
import functools

import jax
import jax.numpy as jnp
from jax import lax
from jax.experimental import pallas as pl
from jax.experimental.pallas import tpu as pltpu
from jax.sharding import PartitionSpec as P

MESH = pl.DeviceIdType.MESH
NX = 4
CAP = 8
BF = jnp.bfloat16
F32 = jnp.float32


def kernel(
    ndp,
    ncuts,
    hid_ref,
    weight_ref,
    term_ref,
    ids_ref,
    comb_ref,
    grad_ref,
    mixed_ref,
    hgrad_ref,
    wgrad_ref,
    out_buf,
    in_buf,
    back_out,
    back_in,
    gath,
    xrelay,
    xpair,
    xnear,
    xfar,
    xsum,
    zhalf,
    zout,
    zin,
    kept,
    a_send,
    a_recv,
    c_send,
    c_recv,
    x_send,
    x_recv,
    h_send,
    h_recv,
    m_send,
    m_recv,
    g_send,
    g_recv,
    gx_send,
    gx_recv,
):
    nz = ncuts // NX
    half = nz // 2
    d = lax.axis_index("dp")
    c = lax.axis_index("cuts")
    z = c // NX
    x = lax.rem(c, NX)
    h = z // half
    k = lax.rem(z, half)
    share, toks = grad_ref.shape
    slots = ndp * CAP

    order = [(o, m) for m in range(1, half) for o in (1, 0)] + [(1, 0), (0, 0)]

    def at(o, m):
        return o * half + m

    def z_block(o, m):
        side = h + o * (1 - 2 * h)
        return side * half + lax.rem(k + m + half, half)

    def cut(zz, xx):
        return zz * NX + lax.rem(xx + NX, NX)

    def dp_peer(i):
        return lax.rem(d + i, ndp)

    barrier = pltpu.get_barrier_semaphore()

    def greet(i, carry):
        pl.semaphore_signal(barrier, inc=1, device_id={"dp": dp_peer(i)}, device_id_type=MESH)
        return carry

    lax.fori_loop(1, ndp, greet, 0)
    near = [cut(z, x + 1), cut(z, x - 1), cut(z_block(1, 0), x)]
    near += [cut(z_block(0, m), x) for m in range(1, half)]
    for peer in near:
        pl.semaphore_signal(barrier, inc=1, device_id={"cuts": peer}, device_id_type=MESH)

    ids0 = ids_ref[0:1, :]
    ids1 = ids_ref[1:2, :]
    label = lax.broadcasted_iota(jnp.int32, (ndp, toks), 0)
    named0 = label == ids0
    named1 = label == ids1
    named = jnp.where(named0 | named1, 1.0, 0.0).astype(BF)
    row = lax.broadcasted_iota(jnp.int32, (toks, toks), 0)
    col = lax.broadcasted_iota(jnp.int32, (toks, toks), 1)
    before = jnp.where(row < col, 1.0, 0.0).astype(BF)
    count = jnp.dot(named, before, preferred_element_type=F32)
    rank0 = jnp.sum(jnp.where(named0, count, 0.0), axis=0, keepdims=True).astype(jnp.int32)
    rank1 = jnp.sum(jnp.where(named1, count, 0.0), axis=0, keepdims=True).astype(jnp.int32)
    place = lax.broadcasted_iota(jnp.int32, (slots, toks), 0)
    pick0 = jnp.where(place == ids0 * CAP + rank0, 1.0, 0.0).astype(BF)
    pick1 = jnp.where(place == ids1 * CAP + rank1, 1.0, 0.0).astype(BF)
    comb0 = comb_ref[0:1, :]
    comb1 = comb_ref[1:2, :]
    grad = grad_ref[...].astype(F32)
    rest = jnp.zeros((128 - share, toks), F32)
    scaled0 = jnp.concatenate([grad * comb0, rest], axis=0).astype(BF)
    scaled1 = jnp.concatenate([grad * comb1, rest], axis=0).astype(BF)
    last = (((1,), (1,)), ((), ()))
    rows = lax.dot_general(pick0, scaled0, last, preferred_element_type=F32) + lax.dot_general(
        pick1, scaled1, last, preferred_element_type=F32
    )
    out_buf[...] = rows.reshape(ndp, CAP, 128).astype(BF)

    pl.semaphore_wait(barrier, ndp - 1 + len(near))

    def dp_copy(src, dst, send, recv, i):
        return pltpu.make_async_remote_copy(
            src_ref=src.at[dp_peer(i)],
            dst_ref=dst.at[d],
            send_sem=send.at[i],
            recv_sem=recv.at[d],
            device_id={"dp": dp_peer(i)},
            device_id_type=MESH,
        )

    def dp_arrival(src, dst, send, recv, i):
        return pltpu.make_async_remote_copy(
            src_ref=src.at[d],
            dst_ref=dst.at[dp_peer(i)],
            send_sem=send.at[i],
            recv_sem=recv.at[dp_peer(i)],
            device_id={"dp": dp_peer(i)},
            device_id_type=MESH,
        )

    def dp_start(src, dst, send, recv):
        def body(i, carry):
            dp_copy(src, dst, send, recv, lax.rem(i + ndp // 2, ndp)).start()
            return carry

        lax.fori_loop(0, ndp // 2, body, 0)
        lax.fori_loop(ndp // 2 + 1, ndp, body, 0)
        dst[d] = src[d]

    def dp_wait_recv(src, dst, send, recv):
        def body(i, carry):
            dp_arrival(src, dst, send, recv, i).wait_recv()
            return carry

        lax.fori_loop(1, ndp, body, 0)

    def dp_wait_send(src, dst, send, recv):
        def body(i, carry):
            dp_copy(src, dst, send, recv, i).wait_send()
            return carry

        lax.fori_loop(1, ndp, body, 0)

    def cuts_copy(src, dst, send, recv, peer):
        return pltpu.make_async_remote_copy(
            src_ref=src,
            dst_ref=dst,
            send_sem=send,
            recv_sem=recv,
            device_id={"cuts": peer},
            device_id_type=MESH,
        )

    def way(o, m):
        return 1 if (o + m) % 2 == 0 else -1

    def rx_far(o, m):
        i, w = at(o, m), way(o, m)
        return cuts_copy(
            term_ref.at[cut(z_block(o, m), x + 2 * w)],
            xrelay.at[i],
            x_send.at[0, i],
            x_recv.at[0, i],
            cut(z, x + w),
        )

    def rx_pair(o, m):
        i, w = at(o, m), way(o, m)
        return cuts_copy(
            xpair.at[i], xfar.at[i], x_send.at[1, i], x_recv.at[1, i], cut(z, x + w)
        )

    def rx_near(o, m):
        i, w = at(o, m), way(o, m)
        return cuts_copy(
            term_ref.at[cut(z_block(o, m), x - w)],
            xnear.at[i],
            x_send.at[2, i],
            x_recv.at[2, i],
            cut(z, x - w),
        )

    def rh_copy(o, m):
        i = at(o, m)
        return cuts_copy(
            xsum.at[i], zhalf.at[i], h_send.at[i], h_recv.at[i], cut(z_block(0, m), x)
        )

    def rm_copy():
        return cuts_copy(zout, zin, m_send.at[0], m_recv.at[0], cut(z_block(1, 0), x))

    def g_own(m):
        return cuts_copy(
            gath.at[c], gath.at[c], g_send.at[m], g_recv.at[m], cut(z_block(0, m), x)
        )

    def g_mirror():
        return cuts_copy(
            gath.at[c],
            gath.at[c],
            g_send.at[half],
            g_recv.at[half],
            cut(z_block(1, 0), x),
        )

    def g_pass(m):
        block = cut(z_block(1, 0), x)
        return cuts_copy(
            gath.at[block],
            gath.at[block],
            g_send.at[half + m],
            g_recv.at[half + m],
            cut(z_block(0, m), x),
        )

    def g_arrival(o, m):
        block = cut(z_block(o, -m), x)
        return cuts_copy(
            gath.at[block],
            gath.at[block],
            g_send.at[at(o, m)],
            g_recv.at[at(o, m)],
            cut(z_block(0, m), x),
        )

    def gx_copy(o, m, w):
        i = at(o, m)
        s = 0 if w == 1 else 1
        block = cut(z_block(o, -m), x)
        return cuts_copy(
            gath.at[block],
            gath.at[block],
            gx_send.at[s, i],
            gx_recv.at[s, i],
            cut(z, x + w),
        )

    def gx_arrival(o, m, w):
        i = at(o, m)
        s = 0 if w == 1 else 1
        block = cut(z_block(o, -m), x - w)
        return cuts_copy(
            gath.at[block],
            gath.at[block],
            gx_send.at[s, i],
            gx_recv.at[s, i],
            cut(z, x + w),
        )

    def gx_relay(o, m):
        i, w = at(o, m), way(o, m)
        block = cut(z_block(o, -m), x - w)
        return cuts_copy(
            gath.at[block],
            gath.at[block],
            gx_send.at[2, i],
            gx_recv.at[2, i],
            cut(z, x + w),
        )

    def gx_relayed(o, m):
        i, w = at(o, m), way(o, m)
        block = cut(z_block(o, -m), x + 2)
        return cuts_copy(
            gath.at[block],
            gath.at[block],
            gx_send.at[2, i],
            gx_recv.at[2, i],
            cut(z, x + w),
        )

    dp_start(out_buf, in_buf, a_send, a_recv)
    for o, m in order:
        rx_far(o, m).start()
        rx_near(o, m).start()

    def relay_pair(o, m):
        i = at(o, m)
        rx_far(o, m).wait_recv()
        own = term_ref[cut(z_block(o, m), x + way(o, m))].astype(F32)
        xpair[i] = (xrelay[i].astype(F32) + own).astype(BF)
        rx_pair(o, m).start()

    def finish_x(o, m):
        i = at(o, m)
        rx_pair(o, m).wait_recv()
        rx_near(o, m).wait_recv()
        total = term_ref[cut(z_block(o, m), x)].astype(F32)
        total = total + xfar[i].astype(F32) + xnear[i].astype(F32)
        if m:
            xsum[i] = total.astype(BF)
            rh_copy(o, m).start()
        else:
            kept[o] = total

    lag = 2
    for n in range(len(order) + lag):
        if n < len(order):
            relay_pair(*order[n])
        if n >= lag:
            finish_x(*order[n - lag])

    dp_wait_recv(out_buf, in_buf, a_send, a_recv)
    arrived = in_buf[...].astype(F32).reshape(slots, 128).T
    gath[c] = arrived[:share].astype(BF)
    g_mirror().start()
    for m in range(1, half):
        g_own(m).start()
    gx_copy(0, 0, 1).start()
    gx_copy(0, 0, -1).start()

    across = kept[1]
    for m in range(1, half):
        rh_copy(1, m).wait_recv()
        across = across + zhalf[at(1, m)].astype(F32)
    zout[...] = across.astype(BF)
    rm_copy().start()
    own = kept[0]
    for m in range(1, half):
        rh_copy(0, m).wait_recv()
        own = own + zhalf[at(0, m)].astype(F32)
    rm_copy().wait_recv()
    own = own + zin[...].astype(F32)
    own = jnp.concatenate([own, jnp.zeros((128 - share, slots), F32)], axis=0)
    back_out[...] = own.T.reshape(ndp, CAP, 128).astype(BF)
    dp_start(back_out, back_in, c_send, c_recv)

    g_arrival(1, 0).wait_recv()
    for m in range(1, half):
        g_pass(m).start()
    gx_copy(1, 0, 1).start()
    gx_copy(1, 0, -1).start()

    turn = [(0, 0), (1, 0)] + [(0, m) for m in range(1, half)] + [(1, m) for m in range(1, half)]
    for n in range(len(turn) + lag):
        if 2 <= n < len(turn):
            o, m = turn[n]
            g_arrival(o, m).wait_recv()
            gx_copy(o, m, 1).start()
            gx_copy(o, m, -1).start()
        if n >= lag:
            o, m = turn[n - lag]
            gx_arrival(o, m, way(o, m)).wait_recv()
            gx_relay(o, m).start()
    for o, m in turn:
        gx_arrival(o, m, -way(o, m)).wait_recv()
        gx_relayed(o, m).wait_recv()

    width = ncuts * share
    full = gath[...].reshape(width, slots)
    hgrad_ref[...] = jnp.dot(weight_ref[...], full, preferred_element_type=F32).T.astype(BF)
    hid_t = hid_ref[...].astype(F32).T.astype(BF)
    step = width // 4
    for n in range(4):
        wgrad_ref[:, n * step : (n + 1) * step] = lax.dot_general(
            hid_t, full[n * step : (n + 1) * step], last, preferred_element_type=F32
        ).astype(BF)

    dp_wait_recv(back_out, back_in, c_send, c_recv)
    expert_rows = back_in[...].astype(F32).reshape(slots, 128).T[:share].astype(BF)
    mixed_ref[...] = (
        comb0 * jnp.dot(expert_rows, pick0, preferred_element_type=F32)
        + comb1 * jnp.dot(expert_rows, pick1, preferred_element_type=F32)
    ).astype(BF)

    dp_wait_send(out_buf, in_buf, a_send, a_recv)
    dp_wait_send(back_out, back_in, c_send, c_recv)
    rm_copy().wait_send()
    g_mirror().wait_send()
    for o, m in order:
        rx_far(o, m).wait_send()
        rx_near(o, m).wait_send()
        rx_pair(o, m).wait_send()
        gx_copy(o, m, 1).wait_send()
        gx_copy(o, m, -1).wait_send()
        gx_relay(o, m).wait_send()
        if m:
            rh_copy(o, m).wait_send()
            (g_pass(m) if o else g_own(m)).wait_send()


def local(hidden, down_weight, expert_ids, combine, out_grad):
    ndp = lax.axis_size("dp")
    ncuts = lax.axis_size("cuts")
    nz = ncuts // NX
    toks, share = out_grad.shape
    hid = hidden[0]
    weight = down_weight[0]
    slots, ff = hid.shape
    width = weight.shape[1]
    terms = lax.dot_general(
        weight, hid, (((0,), (1,)), ((), ())), preferred_element_type=F32
    ).astype(BF)
    vm = pl.BlockSpec(memory_space=pltpu.VMEM)
    dma = pltpu.SemaphoreType.DMA
    block = (share, slots)
    mixed, hgrad, wgrad = pl.pallas_call(
        functools.partial(kernel, ndp, ncuts),
        out_shape=(
            jax.ShapeDtypeStruct((share, toks), BF),
            jax.ShapeDtypeStruct((slots, ff), BF),
            jax.ShapeDtypeStruct((ff, width), BF),
        ),
        in_specs=[vm] * 6,
        out_specs=(vm, vm, vm),
        scratch_shapes=[pltpu.VMEM((ndp, CAP, 128), BF)] * 4
        + [pltpu.VMEM((ncuts,) + block, BF)]
        + [pltpu.VMEM((nz,) + block, BF)] * 6
        + [pltpu.VMEM(block, BF)] * 2
        + [pltpu.VMEM((2,) + block, F32)]
        + [dma((ndp,))] * 4
        + [dma((3, nz))] * 2
        + [dma((nz,))] * 2
        + [dma((1,))] * 2
        + [dma((nz,))] * 2
        + [dma((3, nz))] * 2,
        compiler_params=pltpu.CompilerParams(collective_id=0, has_side_effects=True),
    )(hid, weight, terms.reshape((ncuts,) + block), expert_ids.T, combine.T, out_grad.T)
    return (mixed.T, hgrad[None], wgrad[None])


def solution(mesh):
    return jax.shard_map(
        local,
        mesh=mesh,
        in_specs=(
            P("dp", None, "cuts"),
            P("dp", "cuts", None),
            P("dp", None),
            P("dp", None),
            P("dp", "cuts"),
        ),
        out_specs=(P("dp", "cuts"), P("dp", None, "cuts"), P("dp", "cuts", None)),
        check_vma=False,
    )
```

```python
import functools

import jax
import jax.numpy as jnp
from jax import lax
from jax.experimental import pallas as pl
from jax.experimental.pallas import tpu as pltpu
from jax.sharding import PartitionSpec as P

MESH = pl.DeviceIdType.MESH
NX = 4
CAP = 8
BF = jnp.bfloat16
F32 = jnp.float32


def kernel(
    ndp,
    ncuts,
    hid_ref,
    weight_ref,
    term_ref,
    ids_ref,
    comb_ref,
    grad_ref,
    mixed_ref,
    hgrad_ref,
    wgrad_ref,
    out_buf,
    out_mid,
    out_hop,
    in_buf,
    back_out,
    back_mid,
    back_hop,
    back_in,
    gath,
    xrelay,
    xpair,
    xnear,
    xfar,
    xsum,
    zhalf,
    zout,
    zin,
    kept,
    a_send,
    a_recv,
    c_send,
    c_recv,
    x_send,
    x_recv,
    h_send,
    h_recv,
    m_send,
    m_recv,
    g_send,
    g_recv,
    gx_send,
    gx_recv,
):
    nz = ncuts // NX
    half = nz // 2
    d = lax.axis_index("dp")
    c = lax.axis_index("cuts")
    z = c // NX
    x = lax.rem(c, NX)
    h = z // half
    k = lax.rem(z, half)
    share, toks = grad_ref.shape
    slots = ndp * CAP

    order = [(o, m) for m in range(1, half) for o in (1, 0)] + [(1, 0), (0, 0)]

    def at(o, m):
        return o * half + m

    def z_block(o, m):
        side = h + o * (1 - 2 * h)
        return side * half + lax.rem(k + m + half, half)

    def cut(zz, xx):
        return zz * NX + lax.rem(xx + NX, NX)

    ny = ndp // 4
    y = d // 4
    zh = lax.rem(d // 2, 2)
    co = lax.rem(d, 2)

    def dp_at(yy, zz, cc):
        return (yy * 2 + zz) * 2 + cc

    def y_peer(i):
        return lax.rem(y + i + ny, ny)

    barrier = pltpu.get_barrier_semaphore()

    others = [dp_at(y, 1 - zh, co), dp_at(y, zh, 1 - co)]
    others += [dp_at(y_peer(i), zh, co) for i in range(1, ny)]
    for peer in others:
        pl.semaphore_signal(barrier, inc=1, device_id={"dp": peer}, device_id_type=MESH)
    near = [cut(z, x + 1), cut(z, x - 1), cut(z_block(1, 0), x)]
    near += [cut(z_block(0, m), x) for m in range(1, half)]
    for peer in near:
        pl.semaphore_signal(barrier, inc=1, device_id={"cuts": peer}, device_id_type=MESH)

    ids0 = ids_ref[0:1, :]
    ids1 = ids_ref[1:2, :]
    label = lax.broadcasted_iota(jnp.int32, (ndp, toks), 0)
    named0 = label == ids0
    named1 = label == ids1
    named = jnp.where(named0 | named1, 1.0, 0.0).astype(BF)
    row = lax.broadcasted_iota(jnp.int32, (toks, toks), 0)
    col = lax.broadcasted_iota(jnp.int32, (toks, toks), 1)
    before = jnp.where(row < col, 1.0, 0.0).astype(BF)
    count = jnp.dot(named, before, preferred_element_type=F32)
    rank0 = jnp.sum(jnp.where(named0, count, 0.0), axis=0, keepdims=True).astype(jnp.int32)
    rank1 = jnp.sum(jnp.where(named1, count, 0.0), axis=0, keepdims=True).astype(jnp.int32)
    place = lax.broadcasted_iota(jnp.int32, (slots, toks), 0)
    pick0 = jnp.where(place == ids0 * CAP + rank0, 1.0, 0.0).astype(BF)
    pick1 = jnp.where(place == ids1 * CAP + rank1, 1.0, 0.0).astype(BF)
    comb0 = comb_ref[0:1, :]
    comb1 = comb_ref[1:2, :]
    grad = grad_ref[...].astype(F32)
    rest = jnp.zeros((128 - share, toks), F32)
    scaled0 = jnp.concatenate([grad * comb0, rest], axis=0).astype(BF)
    scaled1 = jnp.concatenate([grad * comb1, rest], axis=0).astype(BF)
    last = (((1,), (1,)), ((), ()))
    rows = lax.dot_general(pick0, scaled0, last, preferred_element_type=F32) + lax.dot_general(
        pick1, scaled1, last, preferred_element_type=F32
    )
    out_buf[...] = rows.reshape(ny, 2, 2, CAP, 128).astype(BF)

    pl.semaphore_wait(barrier, len(others) + len(near))

    class Exchange:
        def __init__(self, src, mid, hop, dst, send, recv):
            self.src, self.mid, self.hop, self.dst = src, mid, hop, dst
            self.send, self.recv = send, recv

        def copy(self, src, dst, n, peer):
            return pltpu.make_async_remote_copy(
                src_ref=src,
                dst_ref=dst,
                send_sem=self.send.at[n],
                recv_sem=self.recv.at[n],
                device_id={"dp": peer},
                device_id_type=MESH,
            )

        def step(self, n, arrival=False):
            far, sibling = dp_at(y, 1 - zh, co), dp_at(y, zh, 1 - co)
            src, mid, hop = self.src, self.mid, self.hop
            if n == 0:
                land = mid.at[:, 1 - zh, co] if arrival else mid.at[:, zh, co]
                return self.copy(src.at[:, 1 - zh, co], land, 0, far)
            if n == 1:
                return self.copy(src.at[:, 1 - zh, 1 - co], hop, 1, far)
            if n == 2:
                land = mid.at[:, zh, 1 - co] if arrival else mid.at[:, zh, co]
                return self.copy(src.at[:, zh, 1 - co], land, 2, sibling)
            if n == 3:
                land = mid.at[:, 1 - zh, 1 - co] if arrival else mid.at[:, 1 - zh, co]
                return self.copy(hop, land, 3, sibling)
            i = n - 3
            land = self.dst.at[y_peer(-i)] if arrival else self.dst.at[y]
            return self.copy(mid.at[y_peer(i)], land, n, dp_at(y_peer(i), zh, co))

        def start(self):
            for n in (1, 0, 2):
                self.step(n).start()
            self.mid[:, zh, co] = self.src[:, zh, co]

        def cross(self):
            self.step(1, True).wait_recv()
            self.step(3).start()

        def spread(self):
            for n in (2, 0, 3):
                self.step(n, True).wait_recv()
            for i in sorted(range(1, ny), key=lambda i: -min(i, ny - i)):
                self.step(3 + i).start()
            self.dst[y] = self.mid[y]

        def wait(self):
            for i in range(1, ny):
                self.step(3 + i, True).wait_recv()

        def done(self):
            for n in range(3 + ny):
                self.step(n).wait_send()

    there = Exchange(out_buf, out_mid, out_hop, in_buf, a_send, a_recv)
    back = Exchange(back_out, back_mid, back_hop, back_in, c_send, c_recv)

    def cuts_copy(src, dst, send, recv, peer):
        return pltpu.make_async_remote_copy(
            src_ref=src,
            dst_ref=dst,
            send_sem=send,
            recv_sem=recv,
            device_id={"cuts": peer},
            device_id_type=MESH,
        )

    def way(o, m):
        return 1 if (o + m) % 2 == 0 else -1

    def rx_far(o, m):
        i, w = at(o, m), way(o, m)
        return cuts_copy(
            term_ref.at[cut(z_block(o, m), x + 2 * w)],
            xrelay.at[i],
            x_send.at[0, i],
            x_recv.at[0, i],
            cut(z, x + w),
        )

    def rx_pair(o, m):
        i, w = at(o, m), way(o, m)
        return cuts_copy(
            xpair.at[i], xfar.at[i], x_send.at[1, i], x_recv.at[1, i], cut(z, x + w)
        )

    def rx_near(o, m):
        i, w = at(o, m), way(o, m)
        return cuts_copy(
            term_ref.at[cut(z_block(o, m), x - w)],
            xnear.at[i],
            x_send.at[2, i],
            x_recv.at[2, i],
            cut(z, x - w),
        )

    def rh_copy(o, m):
        i = at(o, m)
        return cuts_copy(
            xsum.at[i], zhalf.at[i], h_send.at[i], h_recv.at[i], cut(z_block(0, m), x)
        )

    def rm_copy():
        return cuts_copy(zout, zin, m_send.at[0], m_recv.at[0], cut(z_block(1, 0), x))

    def g_own(m):
        return cuts_copy(
            gath.at[c], gath.at[c], g_send.at[m], g_recv.at[m], cut(z_block(0, m), x)
        )

    def g_mirror():
        return cuts_copy(
            gath.at[c],
            gath.at[c],
            g_send.at[half],
            g_recv.at[half],
            cut(z_block(1, 0), x),
        )

    def g_pass(m):
        block = cut(z_block(1, 0), x)
        return cuts_copy(
            gath.at[block],
            gath.at[block],
            g_send.at[half + m],
            g_recv.at[half + m],
            cut(z_block(0, m), x),
        )

    def g_arrival(o, m):
        block = cut(z_block(o, -m), x)
        return cuts_copy(
            gath.at[block],
            gath.at[block],
            g_send.at[at(o, m)],
            g_recv.at[at(o, m)],
            cut(z_block(0, m), x),
        )

    def gx_copy(o, m, w):
        i = at(o, m)
        s = 0 if w == 1 else 1
        block = cut(z_block(o, -m), x)
        return cuts_copy(
            gath.at[block],
            gath.at[block],
            gx_send.at[s, i],
            gx_recv.at[s, i],
            cut(z, x + w),
        )

    def gx_arrival(o, m, w):
        i = at(o, m)
        s = 0 if w == 1 else 1
        block = cut(z_block(o, -m), x - w)
        return cuts_copy(
            gath.at[block],
            gath.at[block],
            gx_send.at[s, i],
            gx_recv.at[s, i],
            cut(z, x + w),
        )

    def gx_relay(o, m):
        i, w = at(o, m), way(o, m)
        block = cut(z_block(o, -m), x - w)
        return cuts_copy(
            gath.at[block],
            gath.at[block],
            gx_send.at[2, i],
            gx_recv.at[2, i],
            cut(z, x + w),
        )

    def gx_relayed(o, m):
        i, w = at(o, m), way(o, m)
        block = cut(z_block(o, -m), x + 2)
        return cuts_copy(
            gath.at[block],
            gath.at[block],
            gx_send.at[2, i],
            gx_recv.at[2, i],
            cut(z, x + w),
        )

    there.start()
    for o, m in order:
        rx_far(o, m).start()
        rx_near(o, m).start()

    def relay_pair(o, m):
        i = at(o, m)
        rx_far(o, m).wait_recv()
        own = term_ref[cut(z_block(o, m), x + way(o, m))].astype(F32)
        xpair[i] = (xrelay[i].astype(F32) + own).astype(BF)
        rx_pair(o, m).start()

    def finish_x(o, m):
        i = at(o, m)
        rx_pair(o, m).wait_recv()
        rx_near(o, m).wait_recv()
        total = term_ref[cut(z_block(o, m), x)].astype(F32)
        total = total + xfar[i].astype(F32) + xnear[i].astype(F32)
        if m:
            xsum[i] = total.astype(BF)
            rh_copy(o, m).start()
        else:
            kept[o] = total

    lag = 2
    for n in range(len(order) + lag):
        if n == len(order) // 2:
            there.cross()
            there.spread()
        if n < len(order):
            relay_pair(*order[n])
        if n >= lag:
            finish_x(*order[n - lag])

    there.wait()
    arrived = in_buf[...].astype(F32).reshape(slots, 128).T
    gath[c] = arrived[:share].astype(BF)
    g_mirror().start()
    for m in range(1, half):
        g_own(m).start()
    gx_copy(0, 0, 1).start()
    gx_copy(0, 0, -1).start()

    across = kept[1]
    for m in range(1, half):
        rh_copy(1, m).wait_recv()
        across = across + zhalf[at(1, m)].astype(F32)
    zout[...] = across.astype(BF)
    rm_copy().start()
    own = kept[0]
    for m in range(1, half):
        rh_copy(0, m).wait_recv()
        own = own + zhalf[at(0, m)].astype(F32)
    rm_copy().wait_recv()
    own = own + zin[...].astype(F32)
    own = jnp.concatenate([own, jnp.zeros((128 - share, slots), F32)], axis=0)
    back_out[...] = own.T.reshape(ny, 2, 2, CAP, 128).astype(BF)
    back.start()

    g_arrival(1, 0).wait_recv()
    for m in range(1, half):
        g_pass(m).start()
    gx_copy(1, 0, 1).start()
    gx_copy(1, 0, -1).start()

    turn = [(0, 0), (1, 0)] + [(0, m) for m in range(1, half)] + [(1, m) for m in range(1, half)]
    for n in range(len(turn) + lag):
        if n == len(turn) // 2 + 1:
            back.cross()
            back.spread()
        if 2 <= n < len(turn):
            o, m = turn[n]
            g_arrival(o, m).wait_recv()
            gx_copy(o, m, 1).start()
            gx_copy(o, m, -1).start()
        if n >= lag:
            o, m = turn[n - lag]
            gx_arrival(o, m, way(o, m)).wait_recv()
            gx_relay(o, m).start()
    for o, m in turn:
        gx_arrival(o, m, -way(o, m)).wait_recv()
        gx_relayed(o, m).wait_recv()

    width = ncuts * share
    full = gath[...].reshape(width, slots)
    hgrad_ref[...] = jnp.dot(weight_ref[...], full, preferred_element_type=F32).T.astype(BF)
    hid_t = hid_ref[...].astype(F32).T.astype(BF)
    step = width // 4
    for n in range(4):
        wgrad_ref[:, n * step : (n + 1) * step] = lax.dot_general(
            hid_t, full[n * step : (n + 1) * step], last, preferred_element_type=F32
        ).astype(BF)

    back.wait()
    expert_rows = back_in[...].astype(F32).reshape(slots, 128).T[:share].astype(BF)
    mixed_ref[...] = (
        comb0 * jnp.dot(expert_rows, pick0, preferred_element_type=F32)
        + comb1 * jnp.dot(expert_rows, pick1, preferred_element_type=F32)
    ).astype(BF)

    there.done()
    back.done()
    rm_copy().wait_send()
    g_mirror().wait_send()
    for o, m in order:
        rx_far(o, m).wait_send()
        rx_near(o, m).wait_send()
        rx_pair(o, m).wait_send()
        gx_copy(o, m, 1).wait_send()
        gx_copy(o, m, -1).wait_send()
        gx_relay(o, m).wait_send()
        if m:
            rh_copy(o, m).wait_send()
            (g_pass(m) if o else g_own(m)).wait_send()


def local(hidden, down_weight, expert_ids, combine, out_grad):
    ndp = lax.axis_size("dp")
    ncuts = lax.axis_size("cuts")
    nz = ncuts // NX
    toks, share = out_grad.shape
    hid = hidden[0]
    weight = down_weight[0]
    slots, ff = hid.shape
    width = weight.shape[1]
    terms = lax.dot_general(
        weight, hid, (((0,), (1,)), ((), ())), preferred_element_type=F32
    ).astype(BF)
    vm = pl.BlockSpec(memory_space=pltpu.VMEM)
    dma = pltpu.SemaphoreType.DMA
    block = (share, slots)
    mixed, hgrad, wgrad = pl.pallas_call(
        functools.partial(kernel, ndp, ncuts),
        out_shape=(
            jax.ShapeDtypeStruct((share, toks), BF),
            jax.ShapeDtypeStruct((slots, ff), BF),
            jax.ShapeDtypeStruct((ff, width), BF),
        ),
        in_specs=[vm] * 6,
        out_specs=(vm, vm, vm),
        scratch_shapes=[
            pltpu.VMEM((ndp // 4, 2, 2, CAP, 128), BF),
            pltpu.VMEM((ndp // 4, 2, 2, CAP, 128), BF),
            pltpu.VMEM((ndp // 4, CAP, 128), BF),
            pltpu.VMEM((ndp // 4, 2, 2, CAP, 128), BF),
        ]
        * 2
        + [pltpu.VMEM((ncuts,) + block, BF)]
        + [pltpu.VMEM((nz,) + block, BF)] * 6
        + [pltpu.VMEM(block, BF)] * 2
        + [pltpu.VMEM((2,) + block, F32)]
        + [dma((ndp // 4 + 3,))] * 4
        + [dma((3, nz))] * 2
        + [dma((nz,))] * 2
        + [dma((1,))] * 2
        + [dma((nz,))] * 2
        + [dma((3, nz))] * 2,
        compiler_params=pltpu.CompilerParams(collective_id=0, has_side_effects=True),
    )(hid, weight, terms.reshape((ncuts,) + block), expert_ids.T, combine.T, out_grad.T)
    return (mixed.T, hgrad[None], wgrad[None])


def solution(mesh):
    return jax.shard_map(
        local,
        mesh=mesh,
        in_specs=(
            P("dp", None, "cuts"),
            P("dp", "cuts", None),
            P("dp", None),
            P("dp", None),
            P("dp", "cuts"),
        ),
        out_specs=(P("dp", "cuts"), P("dp", None, "cuts"), P("dp", "cuts", None)),
        check_vma=False,
    )
```

```python
import functools

import jax
import jax.numpy as jnp
from jax import lax
from jax.experimental import pallas as pl
from jax.experimental.pallas import tpu as pltpu
from jax.sharding import PartitionSpec as P

MESH = pl.DeviceIdType.MESH
NX = 4
CAP = 8
BF = jnp.bfloat16
F32 = jnp.float32


def kernel(
    ndp,
    ncuts,
    hid_ref,
    weight_ref,
    ids_ref,
    comb_ref,
    grad_ref,
    mixed_ref,
    hgrad_ref,
    wgrad_ref,
    term_ref,
    out_buf,
    out_mid,
    out_hop,
    in_buf,
    back_out,
    back_mid,
    back_hop,
    back_in,
    gath,
    xrelay,
    xpair,
    xnear,
    xfar,
    xsum,
    zhalf,
    zout,
    zin,
    kept,
    a_send,
    a_recv,
    c_send,
    c_recv,
    x_send,
    x_recv,
    h_send,
    h_recv,
    m_send,
    m_recv,
    g_send,
    g_recv,
    gx_send,
    gx_recv,
):
    nz = ncuts // NX
    half = nz // 2
    d = lax.axis_index("dp")
    c = lax.axis_index("cuts")
    z = c // NX
    x = lax.rem(c, NX)
    h = z // half
    k = lax.rem(z, half)
    share, toks = grad_ref.shape
    slots = ndp * CAP

    order = [(o, m) for m in range(1, half) for o in (1, 0)] + [(1, 0), (0, 0)]

    def at(o, m):
        return o * half + m

    def z_block(o, m):
        side = h + o * (1 - 2 * h)
        return side * half + lax.rem(k + m + half, half)

    def cut(zz, xx):
        return zz * NX + lax.rem(xx + NX, NX)

    ny = ndp // 4
    y = d // 4
    zh = lax.rem(d // 2, 2)
    co = lax.rem(d, 2)

    def dp_at(yy, zz, cc):
        return (yy * 2 + zz) * 2 + cc

    def y_peer(i):
        return lax.rem(y + i + ny, ny)

    barrier = pltpu.get_barrier_semaphore()

    others = [dp_at(y, 1 - zh, co), dp_at(y, zh, 1 - co)]
    others += [dp_at(y_peer(i), zh, co) for i in range(1, ny)]
    for peer in others:
        pl.semaphore_signal(barrier, inc=1, device_id={"dp": peer}, device_id_type=MESH)
    near = [cut(z, x + 1), cut(z, x - 1), cut(z_block(1, 0), x)]
    near += [cut(z_block(0, m), x) for m in range(1, half)]
    for peer in near:
        pl.semaphore_signal(barrier, inc=1, device_id={"cuts": peer}, device_id_type=MESH)

    ids0 = ids_ref[0:1, :]
    ids1 = ids_ref[1:2, :]
    label = lax.broadcasted_iota(jnp.int32, (ndp, toks), 0)
    named0 = label == ids0
    named1 = label == ids1
    named = jnp.where(named0 | named1, 1.0, 0.0).astype(BF)
    row = lax.broadcasted_iota(jnp.int32, (toks, toks), 0)
    col = lax.broadcasted_iota(jnp.int32, (toks, toks), 1)
    before = jnp.where(row < col, 1.0, 0.0).astype(BF)
    count = jnp.dot(named, before, preferred_element_type=F32)
    rank0 = jnp.sum(jnp.where(named0, count, 0.0), axis=0, keepdims=True).astype(jnp.int32)
    rank1 = jnp.sum(jnp.where(named1, count, 0.0), axis=0, keepdims=True).astype(jnp.int32)
    place = lax.broadcasted_iota(jnp.int32, (slots, toks), 0)
    pick0 = jnp.where(place == ids0 * CAP + rank0, 1.0, 0.0).astype(BF)
    pick1 = jnp.where(place == ids1 * CAP + rank1, 1.0, 0.0).astype(BF)
    comb0 = comb_ref[0:1, :]
    comb1 = comb_ref[1:2, :]
    grad = grad_ref[...].astype(F32)
    rest = jnp.zeros((128 - share, toks), F32)
    scaled0 = jnp.concatenate([grad * comb0, rest], axis=0).astype(BF)
    scaled1 = jnp.concatenate([grad * comb1, rest], axis=0).astype(BF)
    last = (((1,), (1,)), ((), ()))
    rows = lax.dot_general(pick0, scaled0, last, preferred_element_type=F32) + lax.dot_general(
        pick1, scaled1, last, preferred_element_type=F32
    )
    out_buf[...] = rows.reshape(ny, 2, 2, CAP, 128).astype(BF)

    hid_t = hid_ref[...].astype(F32).T.astype(BF)
    width = ncuts * share
    step = width // 4
    for n in range(4):
        term = lax.dot_general(
            weight_ref[:, n * step : (n + 1) * step],
            hid_t,
            (((0,), (0,)), ((), ())),
            preferred_element_type=F32,
        )
        term_ref[n * (ncuts // 4) : (n + 1) * (ncuts // 4)] = term.astype(BF).reshape(
            ncuts // 4, share, slots
        )

    pl.semaphore_wait(barrier, len(others) + len(near))

    class Exchange:
        def __init__(self, src, mid, hop, dst, send, recv):
            self.src, self.mid, self.hop, self.dst = src, mid, hop, dst
            self.send, self.recv = send, recv

        def copy(self, src, dst, n, peer):
            return pltpu.make_async_remote_copy(
                src_ref=src,
                dst_ref=dst,
                send_sem=self.send.at[n],
                recv_sem=self.recv.at[n],
                device_id={"dp": peer},
                device_id_type=MESH,
            )

        def step(self, n, arrival=False):
            far, sibling = dp_at(y, 1 - zh, co), dp_at(y, zh, 1 - co)
            src, mid, hop = self.src, self.mid, self.hop
            if n == 0:
                land = mid.at[:, 1 - zh, co] if arrival else mid.at[:, zh, co]
                return self.copy(src.at[:, 1 - zh, co], land, 0, far)
            if n == 1:
                return self.copy(src.at[:, 1 - zh, 1 - co], hop, 1, far)
            if n == 2:
                land = mid.at[:, zh, 1 - co] if arrival else mid.at[:, zh, co]
                return self.copy(src.at[:, zh, 1 - co], land, 2, sibling)
            if n == 3:
                land = mid.at[:, 1 - zh, 1 - co] if arrival else mid.at[:, 1 - zh, co]
                return self.copy(hop, land, 3, sibling)
            i = n - 3
            land = self.dst.at[y_peer(-i)] if arrival else self.dst.at[y]
            return self.copy(mid.at[y_peer(i)], land, n, dp_at(y_peer(i), zh, co))

        def start(self):
            for n in (1, 0, 2):
                self.step(n).start()
            self.mid[:, zh, co] = self.src[:, zh, co]

        def cross(self):
            self.step(1, True).wait_recv()
            self.step(3).start()

        def spread(self):
            for n in (2, 0, 3):
                self.step(n, True).wait_recv()
            for i in sorted(range(1, ny), key=lambda i: -min(i, ny - i)):
                self.step(3 + i).start()
            self.dst[y] = self.mid[y]

        def wait(self):
            for i in range(1, ny):
                self.step(3 + i, True).wait_recv()

        def done(self):
            for n in range(3 + ny):
                self.step(n).wait_send()

    there = Exchange(out_buf, out_mid, out_hop, in_buf, a_send, a_recv)
    back = Exchange(back_out, back_mid, back_hop, back_in, c_send, c_recv)

    def cuts_copy(src, dst, send, recv, peer):
        return pltpu.make_async_remote_copy(
            src_ref=src,
            dst_ref=dst,
            send_sem=send,
            recv_sem=recv,
            device_id={"cuts": peer},
            device_id_type=MESH,
        )

    def way(o, m):
        return 1 if (o + m) % 2 == 0 else -1

    def rx_far(o, m):
        i, w = at(o, m), way(o, m)
        return cuts_copy(
            term_ref.at[cut(z_block(o, m), x + 2 * w)],
            xrelay.at[i],
            x_send.at[0, i],
            x_recv.at[0, i],
            cut(z, x + w),
        )

    def rx_pair(o, m):
        i, w = at(o, m), way(o, m)
        return cuts_copy(
            xpair.at[i], xfar.at[i], x_send.at[1, i], x_recv.at[1, i], cut(z, x + w)
        )

    def rx_near(o, m):
        i, w = at(o, m), way(o, m)
        return cuts_copy(
            term_ref.at[cut(z_block(o, m), x - w)],
            xnear.at[i],
            x_send.at[2, i],
            x_recv.at[2, i],
            cut(z, x - w),
        )

    def rh_copy(o, m):
        i = at(o, m)
        return cuts_copy(
            xsum.at[i], zhalf.at[i], h_send.at[i], h_recv.at[i], cut(z_block(0, m), x)
        )

    def rm_copy():
        return cuts_copy(zout, zin, m_send.at[0], m_recv.at[0], cut(z_block(1, 0), x))

    def g_own(m):
        return cuts_copy(
            gath.at[c], gath.at[c], g_send.at[m], g_recv.at[m], cut(z_block(0, m), x)
        )

    def g_mirror():
        return cuts_copy(
            gath.at[c],
            gath.at[c],
            g_send.at[half],
            g_recv.at[half],
            cut(z_block(1, 0), x),
        )

    def g_pass(m):
        block = cut(z_block(1, 0), x)
        return cuts_copy(
            gath.at[block],
            gath.at[block],
            g_send.at[half + m],
            g_recv.at[half + m],
            cut(z_block(0, m), x),
        )

    def g_arrival(o, m):
        block = cut(z_block(o, -m), x)
        return cuts_copy(
            gath.at[block],
            gath.at[block],
            g_send.at[at(o, m)],
            g_recv.at[at(o, m)],
            cut(z_block(0, m), x),
        )

    def gx_copy(o, m, w):
        i = at(o, m)
        s = 0 if w == 1 else 1
        block = cut(z_block(o, -m), x)
        return cuts_copy(
            gath.at[block],
            gath.at[block],
            gx_send.at[s, i],
            gx_recv.at[s, i],
            cut(z, x + w),
        )

    def gx_arrival(o, m, w):
        i = at(o, m)
        s = 0 if w == 1 else 1
        block = cut(z_block(o, -m), x - w)
        return cuts_copy(
            gath.at[block],
            gath.at[block],
            gx_send.at[s, i],
            gx_recv.at[s, i],
            cut(z, x + w),
        )

    def gx_relay(o, m):
        i, w = at(o, m), way(o, m)
        block = cut(z_block(o, -m), x - w)
        return cuts_copy(
            gath.at[block],
            gath.at[block],
            gx_send.at[2, i],
            gx_recv.at[2, i],
            cut(z, x + w),
        )

    def gx_relayed(o, m):
        i, w = at(o, m), way(o, m)
        block = cut(z_block(o, -m), x + 2)
        return cuts_copy(
            gath.at[block],
            gath.at[block],
            gx_send.at[2, i],
            gx_recv.at[2, i],
            cut(z, x + w),
        )

    there.start()
    for o, m in order:
        rx_far(o, m).start()
        rx_near(o, m).start()

    def relay_pair(o, m):
        i = at(o, m)
        rx_far(o, m).wait_recv()
        own = term_ref[cut(z_block(o, m), x + way(o, m))].astype(F32)
        xpair[i] = (xrelay[i].astype(F32) + own).astype(BF)
        rx_pair(o, m).start()

    def finish_x(o, m):
        i = at(o, m)
        rx_pair(o, m).wait_recv()
        rx_near(o, m).wait_recv()
        total = term_ref[cut(z_block(o, m), x)].astype(F32)
        total = total + xfar[i].astype(F32) + xnear[i].astype(F32)
        if m:
            xsum[i] = total.astype(BF)
            rh_copy(o, m).start()
        else:
            kept[o] = total

    lag = 2
    for n in range(len(order) + lag):
        if n == len(order) // 2:
            there.cross()
            there.spread()
        if n < len(order):
            relay_pair(*order[n])
        if n >= lag:
            finish_x(*order[n - lag])

    there.wait()
    arrived = in_buf[...].astype(F32).reshape(slots, 128).T
    gath[c] = arrived[:share].astype(BF)
    g_mirror().start()
    for m in range(1, half):
        g_own(m).start()
    gx_copy(0, 0, 1).start()
    gx_copy(0, 0, -1).start()

    across = kept[1]
    for m in range(1, half):
        rh_copy(1, m).wait_recv()
        across = across + zhalf[at(1, m)].astype(F32)
    zout[...] = across.astype(BF)
    rm_copy().start()
    own = kept[0]
    for m in range(1, half):
        rh_copy(0, m).wait_recv()
        own = own + zhalf[at(0, m)].astype(F32)
    rm_copy().wait_recv()
    own = own + zin[...].astype(F32)
    own = jnp.concatenate([own, jnp.zeros((128 - share, slots), F32)], axis=0)
    back_out[...] = own.T.reshape(ny, 2, 2, CAP, 128).astype(BF)
    back.start()

    g_arrival(1, 0).wait_recv()
    for m in range(1, half):
        g_pass(m).start()
    gx_copy(1, 0, 1).start()
    gx_copy(1, 0, -1).start()

    turn = [(0, 0), (1, 0)] + [(0, m) for m in range(1, half)] + [(1, m) for m in range(1, half)]
    for n in range(len(turn) + lag):
        if n == len(turn) // 2 + 1:
            back.cross()
            back.spread()
        if 2 <= n < len(turn):
            o, m = turn[n]
            g_arrival(o, m).wait_recv()
            gx_copy(o, m, 1).start()
            gx_copy(o, m, -1).start()
        if n >= lag:
            o, m = turn[n - lag]
            gx_arrival(o, m, way(o, m)).wait_recv()
            gx_relay(o, m).start()
    for o, m in turn:
        gx_arrival(o, m, -way(o, m)).wait_recv()
        gx_relayed(o, m).wait_recv()

    full = gath[...].reshape(width, slots)
    hgrad_ref[...] = jnp.dot(weight_ref[...], full, preferred_element_type=F32).T.astype(BF)
    for n in range(4):
        wgrad_ref[:, n * step : (n + 1) * step] = lax.dot_general(
            hid_t, full[n * step : (n + 1) * step], last, preferred_element_type=F32
        ).astype(BF)

    back.wait()
    expert_rows = back_in[...].astype(F32).reshape(slots, 128).T[:share].astype(BF)
    mixed_ref[...] = (
        comb0 * jnp.dot(expert_rows, pick0, preferred_element_type=F32)
        + comb1 * jnp.dot(expert_rows, pick1, preferred_element_type=F32)
    ).astype(BF)

    there.done()
    back.done()
    rm_copy().wait_send()
    g_mirror().wait_send()
    for o, m in order:
        rx_far(o, m).wait_send()
        rx_near(o, m).wait_send()
        rx_pair(o, m).wait_send()
        gx_copy(o, m, 1).wait_send()
        gx_copy(o, m, -1).wait_send()
        gx_relay(o, m).wait_send()
        if m:
            rh_copy(o, m).wait_send()
            (g_pass(m) if o else g_own(m)).wait_send()


def local(hidden, down_weight, expert_ids, combine, out_grad):
    ndp = lax.axis_size("dp")
    ncuts = lax.axis_size("cuts")
    nz = ncuts // NX
    toks, share = out_grad.shape
    hid = hidden[0]
    weight = down_weight[0]
    slots, ff = hid.shape
    width = weight.shape[1]
    vm = pl.BlockSpec(memory_space=pltpu.VMEM)
    dma = pltpu.SemaphoreType.DMA
    block = (share, slots)
    mixed, hgrad, wgrad = pl.pallas_call(
        functools.partial(kernel, ndp, ncuts),
        out_shape=(
            jax.ShapeDtypeStruct((share, toks), BF),
            jax.ShapeDtypeStruct((slots, ff), BF),
            jax.ShapeDtypeStruct((ff, width), BF),
        ),
        in_specs=[vm] * 5,
        out_specs=(vm, vm, vm),
        scratch_shapes=[pltpu.VMEM((ncuts,) + block, BF)]
        + [
            pltpu.VMEM((ndp // 4, 2, 2, CAP, 128), BF),
            pltpu.VMEM((ndp // 4, 2, 2, CAP, 128), BF),
            pltpu.VMEM((ndp // 4, CAP, 128), BF),
            pltpu.VMEM((ndp // 4, 2, 2, CAP, 128), BF),
        ]
        * 2
        + [pltpu.VMEM((ncuts,) + block, BF)]
        + [pltpu.VMEM((nz,) + block, BF)] * 6
        + [pltpu.VMEM(block, BF)] * 2
        + [pltpu.VMEM((2,) + block, F32)]
        + [dma((ndp // 4 + 3,))] * 4
        + [dma((3, nz))] * 2
        + [dma((nz,))] * 2
        + [dma((1,))] * 2
        + [dma((nz,))] * 2
        + [dma((3, nz))] * 2,
        compiler_params=pltpu.CompilerParams(collective_id=0, has_side_effects=True),
    )(hid, weight, expert_ids.T, combine.T, out_grad.T)
    return (mixed.T, hgrad[None], wgrad[None])


def solution(mesh):
    return jax.shard_map(
        local,
        mesh=mesh,
        in_specs=(
            P("dp", None, "cuts"),
            P("dp", "cuts", None),
            P("dp", None),
            P("dp", None),
            P("dp", "cuts"),
        ),
        out_specs=(P("dp", "cuts"), P("dp", None, "cuts"), P("dp", "cuts", None)),
        check_vma=False,
    )
```
